32 devices in a mesh: sample: 2 (over y), region: 4 (over x, core), sub: 4 (over z).
Axes of the slice: x: 2, y: 2, z: 4, core: 2. Of those that a mesh axis runs over, the one named last changes fastest.
Arguments:
- densities: bfloat16 [4096, 128], P(('sample', 'region', 'sub')), parts along dimension 0, may hold values from -6 to 6
- cluster_size: int32 [32], P('sample'), parts along dimension 0, may hold values from 1 to 128, 1365 in all
- near_block: bfloat16 [4096, 512], P(('sample', 'region', 'sub')), parts along dimension 0, may hold values from -0.25 to 0.25
- row_factor: bfloat16 [4096, 512], P(('sample', 'region', 'sub')), parts along dimension 0, may hold values from -0.375 to 0.375
- column_factor: bfloat16 [512, 4096], P(None, ('sample', 'region', 'sub')), parts along dimension 1, may hold values from -0.5 to 0.5
Outputs:
- applied: float32 [4096, 128], P(('sample', 'region', 'sub')), parts along dimension 0
The draws below stay inside these ranges and needn't reach their ends.
There are 2 independent parts, one for each index of `sample`. The reference program is written for one: setup_inputs(seed, part) draws one part's arguments, and reference() takes and returns one part's arrays. A program takes and returns all parts, laid end to end along the dimension named above; each array names one. Nothing has to cross between parts.
Inputs may be any that keep to these rules, and one draw needn't show every extreme that they name: `cluster_size`: sizes of the 16 clusters, summing to 1365, with some cluster of exactly 128.
All inputs are finite; a program needn't handle non-finite values.
Results may differ from the reference program's by a relative error of at most 0.0022.
Values may be sent and summed in bfloat16 or wider, within the bound.
No kernel may reach another device: no remote copies, remote signals or barrier semaphores. Data moves between devices by JAX's collectives and lax.ppermute only.
A program may use at most 64 MiB of HBM per device.

```python
import math
import jax
import jax.numpy as jnp
import numpy as np
from jax import lax

CL = 128
LOADS = 128
RANK = 32
CLUSTERS = 16
ROWS = 2048
N_REGION = 4
N_SUB = 4


def strengthened(array, rng, source, target, parts, factor):
    def block_of(dim):
        return (jnp.arange(array.shape[dim]) // (array.shape[dim] // parts)).reshape((-1,) + (1,) * (array.ndim - 1 - dim))

    first = jax.random.permutation(rng, parts)[block_of(target)]
    second = (block_of(target) + parts // 2) % parts
    return jnp.where((block_of(source) == first) | (block_of(source) == second), factor * array, array)


def shard_levels(own_key, shape, split, least, top_value):
    loudness = 1.0
    for axis_at, blocks in split:
        steps = jax.random.uniform(jax.random.fold_in(jax.random.fold_in(own_key, 6), axis_at), (blocks,), jnp.float32, least / len(split), top_value / len(split))
        loudness = loudness * jnp.repeat(jnp.exp(steps), shape[axis_at] // blocks).reshape((-1,) + (1,) * (len(shape) - 1 - axis_at))
    return loudness


def split_up(amount, total, most, lean):
    portions = [(1 << 20) // math.isqrt(grade ** lean) + 1 for grade in range(2, amount + 1)]
    rest, counts = total - most - (amount - 1), [1] * (amount - 1)
    while rest > 0:
        candidates = [i for i in range(amount - 1) if counts[i] < most]
        whole, remaining = sum([portions[i] for i in candidates]), rest
        for i in candidates:
            addition = min(most - counts[i], max(1, remaining * portions[i] // whole), rest)
            counts[i] = counts[i] + addition
            rest = rest - addition
    return np.array([most] + counts)


def ragged_sizes(stream_key, number_of, total, reach, lean):
    if number_of == 2:
        one = jax.random.randint(stream_key, (), max(1, total - reach), min(reach, total - 1) + 1)
        return jnp.stack([one, total - one])
    tallies = jnp.asarray(split_up(number_of, total, reach, lean), jnp.int32)
    couples = (number_of - 1) // 2
    source_of, sink = tallies[1:1 + 2 * couples:2], tallies[2:2 + 2 * couples:2]
    margin = jnp.minimum(source_of - 1, reach - sink)
    shifted = jax.random.randint(jax.random.fold_in(stream_key, 1), (couples,), 0, 1 << 20) % (margin + 1)
    tallies = tallies.at[1:1 + 2 * couples:2].set(source_of - shifted).at[2:2 + 2 * couples:2].set(sink + shifted)
    return tallies[jax.random.permutation(jax.random.fold_in(stream_key, 2), number_of)]


def noise(rng, dims, width, bound, cuts=(), held_as=jnp.bfloat16):
    entries = jax.random.normal(rng, dims, jnp.float32) * width
    if len(cuts) > 0:
        entries = shard_levels(rng, dims, cuts, -0.22, 0.18) * entries
    return jnp.clip(entries, min=-bound, max=bound).astype(held_as)


def noise_with(rng, shape, width, reach, split, heavy, held_as=jnp.bfloat16):
    array = width * jax.random.normal(rng, shape, jnp.float32)
    if split:
        array = array * shard_levels(rng, shape, split, -0.22, 0.18)
    return jnp.clip(strengthened(array, jax.random.fold_in(rng, 3), *heavy), -reach, reach).astype(held_as)


def setup_inputs(seed: int = 0, part: int = 0) -> dict:
    seeds = jax.random.split(jax.random.key(seed), 6)
    own_keys = jax.random.split(jax.random.fold_in(seeds[5], part), 6)
    return {
        "densities": noise(own_keys[0], (ROWS, LOADS), 1.0, 6.0, ((0, 16),)),
        "cluster_size": ragged_sizes(own_keys[1], CLUSTERS, 2 * CLUSTERS * CL // 3, CL, 2).astype(jnp.int32),
        "near_block": noise(own_keys[2], (ROWS, N_SUB * CL), (N_SUB * CL) ** -0.5, 0.25, ((0, 16),)),
        "row_factor": noise_with(own_keys[3], (ROWS, CLUSTERS * RANK), (CLUSTERS * RANK) ** -0.5, 0.375, ((0, 16),), (1, 0, 16, 2.0)),
        "column_factor": noise(own_keys[4], (CLUSTERS * RANK, ROWS), CL ** -0.5, 0.5, ((1, 16),)),
    }


def reference(densities, cluster_size, near_block, row_factor, column_factor):
    row_total, load_count = densities.shape
    cluster_count = N_REGION * N_SUB
    slot_index = jnp.arange(CL, dtype=jnp.int32)
    live_rows = (slot_index[None, :] < cluster_size[:, None]).reshape(row_total, 1)
    masked = jnp.where(live_rows, densities, jnp.zeros_like(densities))
    group_rows = N_SUB * CL
    masked_groups = masked.reshape(N_REGION, group_rows, load_count)
    near_groups = near_block.reshape(N_REGION, group_rows, group_rows)

    def near_one(pair_arrays):
        return jnp.dot(pair_arrays[0], pair_arrays[1], preferred_element_type=jnp.float32)

    near_sum = lax.map(near_one, (near_groups, masked_groups)).reshape(row_total, load_count)
    masked_clusters = masked.reshape(cluster_count, CL, load_count).astype(jnp.float32)
    cluster_region = jnp.arange(cluster_count, dtype=jnp.int32) // N_SUB

    def far_one(target):
        column_rows = lax.dynamic_slice_in_dim(column_factor, target * RANK, RANK, 0)
        column_rows = column_rows.reshape(RANK, cluster_count, CL).astype(jnp.float32)
        coefficients = jnp.einsum("rsc,scn->srn", column_rows, masked_clusters)
        far_flags = cluster_region != target // N_SUB
        coefficients = jnp.where(far_flags[:, None, None], coefficients, jnp.zeros_like(coefficients))
        coefficients = coefficients.astype(jnp.bfloat16)
        row_block = lax.dynamic_slice_in_dim(row_factor, target * CL, CL, 0)
        return jnp.dot(row_block, coefficients.reshape(cluster_count * RANK, load_count), preferred_element_type=jnp.float32)

    far_sum = lax.map(far_one, jnp.arange(cluster_count, dtype=jnp.int32)).reshape(row_total, load_count)
    combined = near_sum + far_sum
    return jnp.where(live_rows, combined, jnp.zeros_like(combined))
```

```python
import functools

import jax
import jax.numpy as jnp
from jax import lax
from jax.experimental import pallas as pl
from jax.experimental.pallas import tpu as pltpu
from jax.sharding import PartitionSpec as P

VMEM = pl.BlockSpec(memory_space=pltpu.VMEM)
HBM = pl.BlockSpec(memory_space=pltpu.HBM)
SMEM = pl.BlockSpec(memory_space=pltpu.SMEM)
GRANT = 8 << 20


def call(body, outs, operands, specs, name, cost):
    return pl.pallas_call(
        body,
        out_shape=outs,
        in_specs=specs,
        out_specs=jax.tree.map(lambda _: VMEM, outs),
        compiler_params=pltpu.CompilerParams(vmem_limit_bytes=GRANT),
        cost_estimate=pl.CostEstimate(flops=cost, bytes_accessed=0, transcendentals=0),
        name=name,
    )(*operands)


def live(size, slots):
    return lax.broadcasted_iota(jnp.int32, (slots, 1), 0) < size


def local(densities, cluster_size, near_block, row_factor, column_factor):
    slots, loads = densities.shape
    groups = lax.axis_size("sub")
    regions = lax.axis_size("region")
    clusters = groups * regions
    rank = row_factor.shape[1] // clusters
    sub_order = sorted(range(1, groups), key=lambda k: (k,))
    far_rows = (regions - 1) * rank
    bf16 = jnp.bfloat16

    def pack(size_hbm, dens_hbm, col_hbm, *refs):
        outs = refs[:groups]
        size_ref, dens_ref, col_ref, sems = refs[groups:]
        copies = [
            pltpu.make_async_copy(source, target, sems.at[i])
            for i, (source, target) in enumerate(
                ((size_hbm, size_ref), (dens_hbm, dens_ref), (col_hbm, col_ref))
            )
        ]
        for copy in copies:
            copy.start()
        sub = lax.axis_index("sub")
        region = lax.axis_index("region")
        own = region * groups + sub
        for copy in copies:
            copy.wait()
        dens = dens_ref[...]
        masked = jnp.where(live(size_ref[own], slots), dens, jnp.zeros_like(dens))
        for step in range(groups):
            out = outs[step]
            base = 0
            if step:
                out[0:slots, :] = dens
                base = slots
            goal = lax.rem(sub + step, groups)
            for hop in range(1, regions):
                row = (lax.rem(region + hop, regions) * groups + goal) * rank
                part = jnp.dot(
                    col_ref[pl.ds(pl.multiple_of(row, rank), rank), :],
                    masked,
                    preferred_element_type=jnp.float32,
                )
                out[base + (hop - 1) * rank : base + hop * rank, :] = part.astype(bf16)

    outs = [jax.ShapeDtypeStruct((far_rows, loads), bf16)] + [
        jax.ShapeDtypeStruct((slots + far_rows, loads), bf16) for _ in range(1, groups)
    ]
    packed = pl.pallas_call(
        pack,
        out_shape=outs,
        in_specs=[HBM] * 3,
        out_specs=[VMEM] * groups,
        scratch_shapes=[
            pltpu.SMEM(cluster_size.shape, cluster_size.dtype),
            pltpu.VMEM(densities.shape, densities.dtype),
            pltpu.VMEM(column_factor.shape, column_factor.dtype),
            pltpu.SemaphoreType.DMA((3,)),
        ],
        compiler_params=pltpu.CompilerParams(vmem_limit_bytes=GRANT),
        name="pack",
    )(*(pltpu.with_memory_space_constraint(x, pltpu.HBM) for x in (cluster_size, densities, column_factor)))

    moved = {}
    for step in sub_order:
        pairs = [(j, (j + step) % groups) for j in range(groups)]
        moved[step] = lax.ppermute(packed[step], "sub", pairs)
    arrived = [moved[step] for step in range(1, groups)]

    def regroup(own_ref, *refs):
        sub = lax.axis_index("sub")
        ins, outs = refs[: groups - 1], refs[groups - 1 :]
        for hop in range(1, regions):
            for step in range(groups):
                source = own_ref if step == 0 else ins[step - 1]
                base = 0 if step == 0 else slots
                origin = lax.rem(sub + groups - step, groups)
                outs[hop - 1][pl.ds(pl.multiple_of(origin * rank, rank), rank), :] = source[
                    base + (hop - 1) * rank : base + hop * rank, :
                ]

    outs = [jax.ShapeDtypeStruct((groups * rank, loads), bf16) for _ in range(1, regions)]
    grouped = call(regroup, outs, (packed[0], *arrived), [VMEM] * groups, "regroup", 1 << 16)

    received = []
    for hop in range(1, regions):
        pairs = [(j, (j + hop) % regions) for j in range(regions)]
        received.append(lax.ppermute(grouped[hop - 1], "region", pairs))

    def near(size_ref, dens_ref, block_ref, *refs):
        ins, out, scratch = refs[: groups - 1], refs[groups - 1], refs[groups]
        sub = lax.axis_index("sub")
        region = lax.axis_index("region")
        for step in range(groups):
            origin = lax.rem(sub + groups - step, groups)
            rows = dens_ref[...] if step == 0 else ins[step - 1][0:slots, :]
            rows = jnp.where(live(size_ref[region * groups + origin], slots), rows, jnp.zeros_like(rows))
            scratch[pl.ds(pl.multiple_of(origin * slots, slots), slots), :] = rows
        out[...] = jnp.dot(block_ref[...], scratch[...], preferred_element_type=jnp.float32)

    near_sum = pl.pallas_call(
        near,
        out_shape=jax.ShapeDtypeStruct((slots, loads), jnp.float32),
        in_specs=[SMEM, VMEM, VMEM] + [VMEM] * (groups - 1),
        out_specs=VMEM,
        scratch_shapes=[pltpu.VMEM((groups * slots, loads), bf16)],
        compiler_params=pltpu.CompilerParams(vmem_limit_bytes=GRANT),
        cost_estimate=pl.CostEstimate(flops=1 << 24, bytes_accessed=1 << 17, transcendentals=0),
        name="near",
    )(cluster_size, densities, near_block, *arrived)

    def finish(size_ref, near_ref, factor_ref, *refs):
        ins, out, scratch = refs[: regions - 1], refs[regions - 1], refs[regions]
        sub = lax.axis_index("sub")
        region = lax.axis_index("region")
        height = groups * rank
        scratch[pl.ds(pl.multiple_of(region * height, height), height), :] = jnp.zeros((height, loads), bf16)
        for hop in range(1, regions):
            origin = lax.rem(region + regions - hop, regions)
            scratch[pl.ds(pl.multiple_of(origin * height, height), height), :] = ins[hop - 1][...]
        far = jnp.dot(factor_ref[...], scratch[...], preferred_element_type=jnp.float32)
        keep = live(size_ref[region * groups + sub], slots)
        out[...] = jnp.where(keep, near_ref[...] + far, 0.0)

    return pl.pallas_call(
        finish,
        out_shape=jax.ShapeDtypeStruct((slots, loads), jnp.float32),
        in_specs=[SMEM, VMEM, VMEM] + [VMEM] * (regions - 1),
        out_specs=VMEM,
        scratch_shapes=[pltpu.VMEM((clusters * rank, loads), bf16)],
        compiler_params=pltpu.CompilerParams(vmem_limit_bytes=GRANT),
        cost_estimate=pl.CostEstimate(flops=1 << 24, bytes_accessed=1 << 17, transcendentals=0),
        name="finish",
    )(cluster_size, near_sum, row_factor, *received)


def solution(mesh):
    spec = P(("sample", "region", "sub"), None)
    return jax.shard_map(
        local,
        mesh=mesh,
        in_specs=(spec, P("sample"), spec, spec, P(None, ("sample", "region", "sub"))),
        out_specs=spec,
        check_vma=False,
    )
```

```python
import jax
import jax.numpy as jnp
from jax import lax
from jax.experimental import pallas as pl
from jax.experimental.pallas import tpu as pltpu
from jax.sharding import PartitionSpec as P


VMEM = pl.BlockSpec(memory_space=pltpu.VMEM)
HBM = pl.BlockSpec(memory_space=pltpu.HBM)
SMEM = pl.BlockSpec(memory_space=pltpu.SMEM)
PARAMS = pltpu.CompilerParams(vmem_limit_bytes=8 << 20)


def cost(flops):
    return pl.CostEstimate(flops=flops, bytes_accessed=0, transcendentals=0)


def at(start, size):
    return pl.ds(pl.multiple_of(start, size), size)


def local(densities, cluster_size, near_block, row_factor, column_factor):
    slots, loads = densities.shape
    groups = lax.axis_size("sub")
    regions = lax.axis_size("region")
    clusters = groups * regions
    rank = row_factor.shape[1] // clusters
    height = groups * rank
    width = (regions - 1) * rank
    bf16, f32 = jnp.bfloat16, jnp.float32
    hops = range(regions - 1, 0, -1)

    def ahead(sub, step):
        return lax.rem(sub + step, groups)

    def behind(sub, step):
        return lax.rem(sub + groups - step, groups)

    def across(region, hop):
        return lax.bitwise_xor(region, jnp.int32(hop))

    def gather(dens, col, *refs):
        outs, (dens_buf, col_buf, sems) = refs[:groups], refs[groups:]
        sub = lax.axis_index("sub")
        region = lax.axis_index("region")
        first = pltpu.make_async_copy(dens, dens_buf, sems.at[0])
        first.start()
        copies = []
        for step in range(groups):
            goal = ahead(sub, step)
            copies.append(pltpu.make_async_copy(col.at[:, goal], col_buf.at[step], sems.at[1]))
            copies[-1].start()
        first.wait()
        for step in range(groups):
            outs[step][0:slots, :] = dens_buf[...]
        for copy in copies:
            copy.wait()
        for step in range(groups):
            for hop in range(1, regions):
                low = slots + (hop - 1) * rank
                outs[step][low : low + rank, :] = col_buf[step, across(region, hop)]

    parcels = pl.pallas_call(
        gather,
        out_shape=[jax.ShapeDtypeStruct((slots + width, loads), bf16)] * groups,
        in_specs=[HBM] * 2,
        out_specs=[VMEM] * groups,
        scratch_shapes=[
            pltpu.VMEM((slots, loads), bf16),
            pltpu.VMEM((groups, regions, rank, slots), bf16),
            pltpu.SemaphoreType.DMA((2,)),
        ],
        compiler_params=PARAMS,
        name="gather",
    )(
        pltpu.with_memory_space_constraint(densities, pltpu.HBM),
        pltpu.with_memory_space_constraint(column_factor.reshape(regions, groups, rank, slots), pltpu.HBM),
    )

    held = [parcels[0]]
    for step in range(1, groups):
        pairs = [(z, (z + step) % groups) for z in range(groups)]
        held.append(lax.ppermute(parcels[step], "sub", pairs))

    def mask(size_ref, group_ref, own_ref):
        sub = lax.axis_index("sub")
        region = lax.axis_index("region")
        slot = lax.broadcasted_iota(jnp.int32, (slots, loads), 0)
        for g in range(groups):
            keep = slot < size_ref[region * groups + g]
            group_ref[g * slots : (g + 1) * slots, :] = jnp.where(keep, 1.0, 0.0).astype(bf16)
        own_ref[...] = jnp.where(slot < size_ref[region * groups + sub], 1.0, 0.0)

    group_mask, own_mask = pl.pallas_call(
        mask,
        out_shape=[
            jax.ShapeDtypeStruct((groups * slots, loads), bf16),
            jax.ShapeDtypeStruct((slots, loads), f32),
        ],
        in_specs=[SMEM],
        out_specs=[VMEM] * 2,
        compiler_params=PARAMS,
        cost_estimate=cost(1 << 20),
        name="mask",
    )(cluster_size)

    def regroup(mask_ref, *refs):
        ins, outs, rows_ref = refs[:groups], refs[groups:-1], refs[-1]
        sub = lax.axis_index("sub")
        for step in range(groups):
            origin = behind(sub, step)
            here = at(origin * slots, slots)
            rows = ins[step][0:slots, :] * mask_ref[here, :]
            rows_ref[here, :] = rows
            part = jnp.dot(ins[step][slots:, :], rows, preferred_element_type=f32).astype(bf16)
            for hop in range(1, regions):
                outs[hop - 1][at(origin * rank, rank), :] = part[(hop - 1) * rank : hop * rank, :]

    *letters, group_rows = pl.pallas_call(
        regroup,
        out_shape=[jax.ShapeDtypeStruct((height, loads), bf16)] * (regions - 1)
        + [jax.ShapeDtypeStruct((groups * slots, loads), bf16)],
        in_specs=[VMEM] * (groups + 1),
        out_specs=[VMEM] * regions,
        compiler_params=PARAMS,
        cost_estimate=cost(1 << 20),
        name="regroup",
    )(group_mask, *held)

    received = {}
    for hop in hops:
        pairs = [(r, r ^ hop) for r in range(regions)]
        received[hop] = lax.ppermute(letters[hop - 1], "region", pairs)

    def near(block_ref, rows_ref, out):
        out[...] = jnp.dot(block_ref[...], rows_ref[...], preferred_element_type=f32)

    near_sum = pl.pallas_call(
        near,
        out_shape=jax.ShapeDtypeStruct((slots, loads), f32),
        in_specs=[VMEM] * 2,
        out_specs=VMEM,
        compiler_params=PARAMS,
        cost_estimate=cost(1 << 24),
        name="near",
    )(near_block, group_rows)

    def finish(mask_ref, near_ref, factor_ref, *refs):
        ins, out, scratch = refs[: regions - 1], refs[regions - 1], refs[regions]
        region = lax.axis_index("region")
        scratch[at(region * height, height), :] = jnp.zeros((height, loads), bf16)
        for hop in range(1, regions):
            scratch[at(across(region, hop) * height, height), :] = ins[hop - 1][...]
        far = jnp.dot(factor_ref[...], scratch[...], preferred_element_type=f32)
        out[...] = jnp.where(mask_ref[...] > 0.0, near_ref[...] + far, 0.0)

    return pl.pallas_call(
        finish,
        out_shape=jax.ShapeDtypeStruct((slots, loads), f32),
        in_specs=[VMEM] * (regions + 2),
        out_specs=VMEM,
        scratch_shapes=[pltpu.VMEM((clusters * rank, loads), bf16)],
        compiler_params=PARAMS,
        cost_estimate=cost(1 << 24),
        name="finish",
    )(own_mask, near_sum, row_factor, *(received[hop] for hop in range(1, regions)))


def solution(mesh):
    spec = P(("sample", "region", "sub"), None)
    return jax.shard_map(
        local,
        mesh=mesh,
        in_specs=(spec, P("sample"), spec, spec, P(None, ("sample", "region", "sub"))),
        out_specs=spec,
        check_vma=False,
    )
```

```python
import jax
import jax.numpy as jnp
from jax import lax
from jax.experimental import pallas as pl
from jax.experimental.pallas import tpu as pltpu
from jax.sharding import PartitionSpec as P


VMEM = pl.BlockSpec(memory_space=pltpu.VMEM)
HBM = pl.BlockSpec(memory_space=pltpu.HBM)
SMEM = pl.BlockSpec(memory_space=pltpu.SMEM)
PARAMS = pltpu.CompilerParams(vmem_limit_bytes=8 << 20)


def cost(flops):
    return pl.CostEstimate(flops=flops, bytes_accessed=0, transcendentals=0)


def at(start, size):
    return pl.ds(pl.multiple_of(start, size), size)


def local(densities, cluster_size, near_block, row_factor, column_factor):
    slots, loads = densities.shape
    groups = lax.axis_size("sub")
    regions = lax.axis_size("region")
    clusters = groups * regions
    rank = row_factor.shape[1] // clusters
    height = groups * rank
    width = (regions - 1) * rank
    bf16, f32 = jnp.bfloat16, jnp.float32
    hops = range(regions - 1, 0, -1)

    def ahead(sub, step):
        return lax.rem(sub + step, groups)

    def behind(sub, step):
        return lax.rem(sub + groups - step, groups)

    def across(region, hop):
        return lax.bitwise_xor(region, jnp.int32(hop))

    def gather(dens, col, *refs):
        outs, (dens_buf, col_buf, sems) = refs[:groups], refs[groups:]
        sub = lax.axis_index("sub")
        region = lax.axis_index("region")
        first = pltpu.make_async_copy(dens, dens_buf, sems.at[0])
        first.start()
        copies = []
        for step in range(groups):
            goal = ahead(sub, step)
            copies.append(pltpu.make_async_copy(col.at[:, goal], col_buf.at[step], sems.at[1]))
            copies[-1].start()
        first.wait()
        for step in range(groups):
            outs[step][0:slots, :] = dens_buf[...]
        for copy in copies:
            copy.wait()
        for step in range(groups):
            for hop in range(1, regions):
                low = slots + (hop - 1) * rank
                outs[step][low : low + rank, :] = col_buf[step, across(region, hop)]

    parcels = pl.pallas_call(
        gather,
        out_shape=[jax.ShapeDtypeStruct((slots + width, loads), bf16)] * groups,
        in_specs=[HBM] * 2,
        out_specs=[VMEM] * groups,
        scratch_shapes=[
            pltpu.VMEM((slots, loads), bf16),
            pltpu.VMEM((groups, regions, rank, slots), bf16),
            pltpu.SemaphoreType.DMA((2,)),
        ],
        compiler_params=PARAMS,
        name="gather",
    )(
        pltpu.with_memory_space_constraint(densities, pltpu.HBM),
        pltpu.with_memory_space_constraint(column_factor.reshape(regions, groups, rank, slots), pltpu.HBM),
    )

    held = [parcels[0]]
    for step in range(1, groups):
        pairs = [(z, (z + step) % groups) for z in range(groups)]
        held.append(lax.ppermute(parcels[step], "sub", pairs))

    def mask(size_ref, group_ref, own_ref):
        sub = lax.axis_index("sub")
        region = lax.axis_index("region")
        slot = lax.broadcasted_iota(jnp.int32, (slots, loads), 0)
        for g in range(groups):
            keep = slot < size_ref[region * groups + g]
            group_ref[g * slots : (g + 1) * slots, :] = jnp.where(keep, 1.0, 0.0).astype(bf16)
        own_ref[...] = jnp.where(slot < size_ref[region * groups + sub], 1.0, 0.0)

    group_mask, own_mask = pl.pallas_call(
        mask,
        out_shape=[
            jax.ShapeDtypeStruct((groups * slots, loads), bf16),
            jax.ShapeDtypeStruct((slots, loads), f32),
        ],
        in_specs=[SMEM],
        out_specs=[VMEM] * 2,
        compiler_params=PARAMS,
        cost_estimate=cost(1 << 20),
        name="mask",
    )(cluster_size)

    def weigh(step, mask_ref, parcel, outs):
        sub = lax.axis_index("sub")
        origin = behind(sub, step)
        rows = parcel[0:slots, :] * mask_ref[at(origin * slots, slots), :]
        part = jnp.dot(parcel[slots:, :], rows, preferred_element_type=f32).astype(bf16)
        for hop in range(1, regions):
            outs[hop - 1][at(origin * rank, rank), :] = part[(hop - 1) * rank : hop * rank, :]

    def regroup(mask_ref, *refs):
        for step in range(groups - 1):
            weigh(step, mask_ref, refs[step], refs[groups - 1 :])

    def complete(mask_ref, parcel, *refs):
        weigh(groups - 1, mask_ref, parcel, refs[regions - 1 :])

    letter_shapes = [jax.ShapeDtypeStruct((height, loads), bf16)] * (regions - 1)
    letters = pl.pallas_call(
        regroup,
        out_shape=letter_shapes,
        in_specs=[VMEM] * groups,
        out_specs=[VMEM] * (regions - 1),
        compiler_params=PARAMS,
        cost_estimate=cost(1 << 20),
        name="regroup",
    )(group_mask, *held[:-1])
    letters = pl.pallas_call(
        complete,
        out_shape=letter_shapes,
        in_specs=[VMEM] * (regions + 1),
        out_specs=[VMEM] * (regions - 1),
        input_output_aliases={hop + 1: hop - 1 for hop in range(1, regions)},
        compiler_params=PARAMS,
        cost_estimate=cost(1 << 20),
        name="complete",
    )(group_mask, held[-1], *letters)

    received = {}
    for hop in hops:
        pairs = [(r, r ^ hop) for r in range(regions)]
        received[hop] = lax.ppermute(letters[hop - 1], "region", pairs)

    late = min(2, regions - 1)
    early = [hop for hop in range(1, regions) if hop != late]

    def far_part(factor_ref, letter, hop):
        start = across(lax.axis_index("region"), hop) * height
        return jnp.dot(factor_ref[:, at(start, height)], letter[...], preferred_element_type=f32)

    def near(block_ref, mask_ref, *refs):
        parcels, out, stack = refs[:groups], refs[groups], refs[groups + 1]
        sub = lax.axis_index("sub")
        for step in range(groups):
            here = at(behind(sub, step) * slots, slots)
            stack[here, :] = parcels[step][0:slots, :] * mask_ref[here, :]
        out[...] = jnp.dot(block_ref[...], stack[...], preferred_element_type=f32)

    near_sum = pl.pallas_call(
        near,
        out_shape=jax.ShapeDtypeStruct((slots, loads), f32),
        in_specs=[VMEM] * (groups + 2),
        out_specs=VMEM,
        scratch_shapes=[pltpu.VMEM((groups * slots, loads), bf16)],
        compiler_params=PARAMS,
        cost_estimate=cost(1 << 24),
        name="near",
    )(near_block, group_mask, *held)

    def gain(near_ref, factor_ref, *refs):
        total = near_ref[...]
        for hop, letter in zip(early, refs):
            total += far_part(factor_ref, letter, hop)
        refs[-1][...] = total

    partial = pl.pallas_call(
        gain,
        out_shape=jax.ShapeDtypeStruct((slots, loads), f32),
        in_specs=[VMEM] * (len(early) + 2),
        out_specs=VMEM,
        compiler_params=PARAMS,
        cost_estimate=cost(1 << 24),
        name="gain",
    )(near_sum, row_factor, *(received[hop] for hop in early))

    def finish(mask_ref, partial_ref, factor_ref, letter, out):
        total = partial_ref[...] + far_part(factor_ref, letter, late)
        out[...] = jnp.where(mask_ref[...] > 0.0, total, 0.0)

    return pl.pallas_call(
        finish,
        out_shape=jax.ShapeDtypeStruct((slots, loads), f32),
        in_specs=[VMEM] * 4,
        out_specs=VMEM,
        compiler_params=PARAMS,
        cost_estimate=cost(1 << 24),
        name="finish",
    )(own_mask, partial, row_factor, received[late])


def solution(mesh):
    spec = P(("sample", "region", "sub"), None)
    return jax.shard_map(
        local,
        mesh=mesh,
        in_specs=(spec, P("sample"), spec, spec, P(None, ("sample", "region", "sub"))),
        out_specs=spec,
        check_vma=False,
    )
```

```python
import jax
import jax.numpy as jnp
from jax import lax
from jax.experimental import pallas as pl
from jax.experimental.pallas import tpu as pltpu
from jax.sharding import PartitionSpec as P


VMEM = pl.BlockSpec(memory_space=pltpu.VMEM)
HBM = pl.BlockSpec(memory_space=pltpu.HBM)
SMEM = pl.BlockSpec(memory_space=pltpu.SMEM)
PARAMS = pltpu.CompilerParams(vmem_limit_bytes=8 << 20)


def cost(flops):
    return pl.CostEstimate(flops=flops, bytes_accessed=0, transcendentals=0)


def at(start, size):
    return pl.ds(pl.multiple_of(start, size), size)


def local(densities, cluster_size, near_block, row_factor, column_factor):
    slots, loads = densities.shape
    groups = lax.axis_size("sub")
    regions = lax.axis_size("region")
    clusters = groups * regions
    rank = row_factor.shape[1] // clusters
    height = groups * rank
    width = (regions - 1) * rank
    bf16, f32 = jnp.bfloat16, jnp.float32
    hops = range(regions - 1, 0, -1)

    def ahead(sub, step):
        return lax.rem(sub + step, groups)

    def behind(sub, step):
        return lax.rem(sub + groups - step, groups)

    def across(region, hop):
        return lax.bitwise_xor(region, jnp.int32(hop))

    def gather(dens, col, *refs):
        outs, (dens_buf, col_buf, sems) = refs[:groups], refs[groups:]
        sub = lax.axis_index("sub")
        region = lax.axis_index("region")
        first = pltpu.make_async_copy(dens, dens_buf, sems.at[0])
        first.start()
        copies = []
        for step in range(groups):
            goal = ahead(sub, step)
            copies.append(pltpu.make_async_copy(col.at[:, goal], col_buf.at[step], sems.at[1]))
            copies[-1].start()
        first.wait()
        for step in range(groups):
            outs[step][0:slots, :] = dens_buf[...]
        for copy in copies:
            copy.wait()
        for step in range(groups):
            for hop in range(1, regions):
                low = slots + (hop - 1) * rank
                outs[step][low : low + rank, :] = col_buf[step, across(region, hop)]

    parcels = pl.pallas_call(
        gather,
        out_shape=[jax.ShapeDtypeStruct((slots + width, loads), bf16)] * groups,
        in_specs=[HBM] * 2,
        out_specs=[VMEM] * groups,
        scratch_shapes=[
            pltpu.VMEM((slots, loads), bf16),
            pltpu.VMEM((groups, regions, rank, slots), bf16),
            pltpu.SemaphoreType.DMA((2,)),
        ],
        compiler_params=PARAMS,
        name="gather",
    )(
        pltpu.with_memory_space_constraint(densities, pltpu.HBM),
        pltpu.with_memory_space_constraint(column_factor.reshape(regions, groups, rank, slots), pltpu.HBM),
    )

    held = [parcels[0]]
    for step in range(1, groups):
        pairs = [(z, (z + step) % groups) for z in range(groups)]
        held.append(lax.ppermute(parcels[step], "sub", pairs))

    def mask(size_ref, group_ref, own_ref):
        sub = lax.axis_index("sub")
        region = lax.axis_index("region")
        slot = lax.broadcasted_iota(jnp.int32, (slots, loads), 0)
        for g in range(groups):
            keep = slot < size_ref[region * groups + g]
            group_ref[g * slots : (g + 1) * slots, :] = jnp.where(keep, 1.0, 0.0).astype(bf16)
        own_ref[...] = jnp.where(slot < size_ref[region * groups + sub], 1.0, 0.0)

    group_mask, own_mask = pl.pallas_call(
        mask,
        out_shape=[
            jax.ShapeDtypeStruct((groups * slots, loads), bf16),
            jax.ShapeDtypeStruct((slots, loads), f32),
        ],
        in_specs=[SMEM],
        out_specs=[VMEM] * 2,
        compiler_params=PARAMS,
        cost_estimate=cost(1 << 20),
        name="mask",
    )(cluster_size)

    def weigh(step, mask_ref, parcel, outs):
        sub = lax.axis_index("sub")
        origin = behind(sub, step)
        rows = parcel[0:slots, :] * mask_ref[at(origin * slots, slots), :]
        part = jnp.dot(parcel[slots:, :], rows, preferred_element_type=f32).astype(bf16)
        for hop in range(1, regions):
            outs[hop - 1][at(origin * rank, rank), :] = part[(hop - 1) * rank : hop * rank, :]

    def regroup(mask_ref, *refs):
        for step in range(groups - 1):
            weigh(step, mask_ref, refs[step], refs[groups - 1 :])

    def complete(mask_ref, parcel, *refs):
        begun, outs = refs[: regions - 1], refs[regions - 1 :]
        for source, out in zip(begun, outs):
            out[...] = source[...]
        weigh(groups - 1, mask_ref, parcel, outs)

    letter_shapes = [jax.ShapeDtypeStruct((height, loads), bf16)] * (regions - 1)
    letters = pl.pallas_call(
        regroup,
        out_shape=letter_shapes,
        in_specs=[VMEM] * groups,
        out_specs=[VMEM] * (regions - 1),
        compiler_params=PARAMS,
        cost_estimate=cost(1 << 20),
        name="regroup",
    )(group_mask, *held[:-1])
    letters = pl.pallas_call(
        complete,
        out_shape=letter_shapes,
        in_specs=[VMEM] * (regions + 1),
        out_specs=[VMEM] * (regions - 1),
        compiler_params=PARAMS,
        cost_estimate=cost(1 << 20),
        name="complete",
    )(group_mask, held[-1], *letters)

    received = {}
    for hop in hops:
        pairs = [(r, r ^ hop) for r in range(regions)]
        received[hop] = lax.ppermute(letters[hop - 1], "region", pairs)

    late = min(2, regions - 1)
    early = [hop for hop in range(1, regions) if hop != late]

    def far_part(factor_ref, letter, hop):
        start = across(lax.axis_index("region"), hop) * height
        return jnp.dot(factor_ref[:, at(start, height)], letter[...], preferred_element_type=f32)

    def near(block_ref, mask_ref, *refs):
        parcels, out, stack = refs[:groups], refs[groups], refs[groups + 1]
        sub = lax.axis_index("sub")
        for step in range(groups):
            here = at(behind(sub, step) * slots, slots)
            stack[here, :] = parcels[step][0:slots, :] * mask_ref[here, :]
        out[...] = jnp.dot(block_ref[...], stack[...], preferred_element_type=f32)

    near_sum = pl.pallas_call(
        near,
        out_shape=jax.ShapeDtypeStruct((slots, loads), f32),
        in_specs=[VMEM] * (groups + 2),
        out_specs=VMEM,
        scratch_shapes=[pltpu.VMEM((groups * slots, loads), bf16)],
        compiler_params=PARAMS,
        cost_estimate=cost(1 << 24),
        name="near",
    )(near_block, group_mask, *held)

    def gain(near_ref, factor_ref, *refs):
        total = near_ref[...]
        for hop, letter in zip(early, refs):
            total += far_part(factor_ref, letter, hop)
        refs[-1][...] = total

    partial = pl.pallas_call(
        gain,
        out_shape=jax.ShapeDtypeStruct((slots, loads), f32),
        in_specs=[VMEM] * (len(early) + 2),
        out_specs=VMEM,
        compiler_params=PARAMS,
        cost_estimate=cost(1 << 24),
        name="gain",
    )(near_sum, row_factor, *(received[hop] for hop in early))

    def finish(mask_ref, partial_ref, factor_ref, letter, out):
        total = partial_ref[...] + far_part(factor_ref, letter, late)
        out[...] = jnp.where(mask_ref[...] > 0.0, total, 0.0)

    return pl.pallas_call(
        finish,
        out_shape=jax.ShapeDtypeStruct((slots, loads), f32),
        in_specs=[VMEM] * 4,
        out_specs=VMEM,
        compiler_params=PARAMS,
        cost_estimate=cost(1 << 24),
        name="finish",
    )(own_mask, partial, row_factor, received[late])


def solution(mesh):
    spec = P(("sample", "region", "sub"), None)
    return jax.shard_map(
        local,
        mesh=mesh,
        in_specs=(spec, P("sample"), spec, spec, P(None, ("sample", "region", "sub"))),
        out_specs=spec,
        check_vma=False,
    )
```

```python
import jax
import jax.numpy as jnp
from jax import lax
from jax.experimental import pallas as pl
from jax.experimental.pallas import tpu as pltpu
from jax.sharding import PartitionSpec as P


VMEM = pl.BlockSpec(memory_space=pltpu.VMEM)
HBM = pl.BlockSpec(memory_space=pltpu.HBM)
SMEM = pl.BlockSpec(memory_space=pltpu.SMEM)
PARAMS = pltpu.CompilerParams(vmem_limit_bytes=8 << 20)


def cost(flops):
    return pl.CostEstimate(flops=flops, bytes_accessed=0, transcendentals=0)


def folded(count):
    odd = list(range(1, count, 2))
    even = list(range(2, count, 2))
    return [0] + odd + even[::-1]


def at(start, size):
    return pl.ds(pl.multiple_of(start, size), size)


def local(densities, cluster_size, near_block, row_factor, column_factor):
    slots, loads = densities.shape
    groups = lax.axis_size("sub")
    regions = lax.axis_size("region")
    clusters = groups * regions
    rank = row_factor.shape[1] // clusters
    height = groups * rank
    width = (regions - 1) * rank
    bf16, f32 = jnp.bfloat16, jnp.float32
    hops = range(regions - 1, 0, -1)

    def ahead(sub, step):
        return lax.rem(sub + step, groups)

    def behind(sub, step):
        return lax.rem(sub + groups - step, groups)

    def across(region, hop):
        return lax.bitwise_xor(region, jnp.int32(hop))

    def pack(size_hbm, dens_hbm, col_hbm, *refs):
        outs, (size, dens, col, found, sems) = refs[:groups], refs[groups:]
        copies = [
            pltpu.make_async_copy(source, target, sems.at[i])
            for i, (source, target) in enumerate(((size_hbm, size), (dens_hbm, dens), (col_hbm, col)))
        ]
        for copy in copies:
            copy.start()
        sub = lax.axis_index("sub")
        region = lax.axis_index("region")
        slot = lax.broadcasted_iota(jnp.int32, (slots, loads), 0)
        for copy in copies[:2]:
            copy.wait()
        rows = dens[...] * jnp.where(slot < size[region * groups + sub], 1.0, 0.0).astype(bf16)
        copies[2].wait()
        for step in range(groups):
            goal = ahead(sub, step)
            for hop in range(1, regions):
                row = across(region, hop) * height + goal * rank
                found[(hop - 1) * rank : hop * rank, :] = col[at(row, rank), :]
            outs[step][...] = jnp.dot(found[...], rows, preferred_element_type=f32).astype(bf16)

    parcels = pl.pallas_call(
        pack,
        out_shape=[jax.ShapeDtypeStruct((width, loads), bf16)] * groups,
        in_specs=[HBM] * 3,
        out_specs=[VMEM] * groups,
        scratch_shapes=[
            pltpu.SMEM(cluster_size.shape, cluster_size.dtype),
            pltpu.VMEM((slots, loads), bf16),
            pltpu.VMEM((clusters * rank, slots), bf16),
            pltpu.VMEM((width, slots), bf16),
            pltpu.SemaphoreType.DMA((3,)),
        ],
        compiler_params=PARAMS,
        name="pack",
    )(*(pltpu.with_memory_space_constraint(x, pltpu.HBM) for x in (cluster_size, densities, column_factor)))

    held = [parcels[0]]
    for step in range(1, groups):
        pairs = [(z, (z + step) % groups) for z in range(groups)]
        held.append(lax.ppermute(parcels[step], "sub", pairs))
    ring = folded(groups)
    nearby = [densities]
    for step in range(1, groups):
        pairs = [(ring[p], ring[(p + step) % groups]) for p in range(groups)]
        nearby.append(lax.ppermute(densities, "sub", pairs))

    def fetch(size_hbm, block_hbm, factor_hbm, group_ref, own_ref, block_ref, factor_ref, size, sems):
        copies = [
            pltpu.make_async_copy(source, target, sems.at[i])
            for i, (source, target) in enumerate(
                ((size_hbm, size), (block_hbm, block_ref), (factor_hbm, factor_ref))
            )
        ]
        for copy in copies:
            copy.start()
        sub = lax.axis_index("sub")
        region = lax.axis_index("region")
        slot = lax.broadcasted_iota(jnp.int32, (slots, loads), 0)
        copies[0].wait()
        for g in range(groups):
            keep = slot < size[region * groups + g]
            group_ref[g * slots : (g + 1) * slots, :] = jnp.where(keep, 1.0, 0.0).astype(bf16)
        own_ref[...] = jnp.where(slot < size[region * groups + sub], 1.0, 0.0)
        for copy in copies[1:]:
            copy.wait()

    group_mask, own_mask, near_block, row_factor = pl.pallas_call(
        fetch,
        out_shape=[
            jax.ShapeDtypeStruct((groups * slots, loads), bf16),
            jax.ShapeDtypeStruct((slots, loads), f32),
            jax.ShapeDtypeStruct(near_block.shape, bf16),
            jax.ShapeDtypeStruct(row_factor.shape, bf16),
        ],
        in_specs=[HBM] * 3,
        out_specs=[VMEM] * 4,
        scratch_shapes=[
            pltpu.SMEM(cluster_size.shape, cluster_size.dtype),
            pltpu.SemaphoreType.DMA((3,)),
        ],
        compiler_params=PARAMS,
        cost_estimate=cost(1 << 20),
        name="fetch",
    )(*(pltpu.with_memory_space_constraint(x, pltpu.HBM) for x in (cluster_size, near_block, row_factor)))

    def regroup(*refs):
        ins, outs = refs[:groups], refs[groups:]
        sub = lax.axis_index("sub")
        for step in range(groups):
            for hop in range(1, regions):
                outs[hop - 1][at(behind(sub, step) * rank, rank), :] = ins[step][(hop - 1) * rank : hop * rank, :]

    letters = pl.pallas_call(
        regroup,
        out_shape=[jax.ShapeDtypeStruct((height, loads), bf16)] * (regions - 1),
        in_specs=[VMEM] * groups,
        out_specs=[VMEM] * (regions - 1),
        compiler_params=PARAMS,
        cost_estimate=cost(1 << 16),
        name="regroup",
    )(*held)

    received = {}
    for hop in hops:
        pairs = [(r, r ^ hop) for r in range(regions)]
        received[hop] = lax.ppermute(letters[hop - 1], "region", pairs)

    late = min(2, regions - 1)
    early = [hop for hop in range(1, regions) if hop != late]

    def far_part(factor_ref, letter, hop):
        start = across(lax.axis_index("region"), hop) * height
        return jnp.dot(factor_ref[:, at(start, height)], letter[...], preferred_element_type=f32)

    def near(block_ref, mask_ref, *refs):
        parcels, out, stack = refs[:groups], refs[groups], refs[groups + 1]
        sub = lax.axis_index("sub")
        for step in range(groups):
            origin = sub
            if step:
                for p in range(groups):
                    origin = jnp.where(sub == ring[p], ring[p - step], origin)
            here = at(origin * slots, slots)
            stack[here, :] = parcels[step][...] * mask_ref[here, :]
        out[...] = jnp.dot(block_ref[...], stack[...], preferred_element_type=f32)

    near_sum = pl.pallas_call(
        near,
        out_shape=jax.ShapeDtypeStruct((slots, loads), f32),
        in_specs=[VMEM] * (groups + 2),
        out_specs=VMEM,
        scratch_shapes=[pltpu.VMEM((groups * slots, loads), bf16)],
        compiler_params=PARAMS,
        cost_estimate=cost(1 << 24),
        name="near",
    )(near_block, group_mask, *nearby)

    def gain(near_ref, factor_ref, *refs):
        total = near_ref[...]
        for hop, letter in zip(early, refs):
            total += far_part(factor_ref, letter, hop)
        refs[-1][...] = total

    partial = pl.pallas_call(
        gain,
        out_shape=jax.ShapeDtypeStruct((slots, loads), f32),
        in_specs=[VMEM] * (len(early) + 2),
        out_specs=VMEM,
        compiler_params=PARAMS,
        cost_estimate=cost(1 << 24),
        name="gain",
    )(near_sum, row_factor, *(received[hop] for hop in early))

    def finish(mask_ref, partial_ref, factor_ref, letter, out):
        total = partial_ref[...] + far_part(factor_ref, letter, late)
        out[...] = jnp.where(mask_ref[...] > 0.0, total, 0.0)

    return pl.pallas_call(
        finish,
        out_shape=jax.ShapeDtypeStruct((slots, loads), f32),
        in_specs=[VMEM] * 4,
        out_specs=VMEM,
        compiler_params=PARAMS,
        cost_estimate=cost(1 << 24),
        name="finish",
    )(own_mask, partial, row_factor, received[late])


def solution(mesh):
    spec = P(("sample", "region", "sub"), None)
    return jax.shard_map(
        local,
        mesh=mesh,
        in_specs=(spec, P("sample"), spec, spec, P(None, ("sample", "region", "sub"))),
        out_specs=spec,
        check_vma=False,
    )
```

```python
import jax
import jax.numpy as jnp
from jax import lax
from jax.experimental import pallas as pl
from jax.experimental.pallas import tpu as pltpu
from jax.sharding import PartitionSpec as P


VMEM = pl.BlockSpec(memory_space=pltpu.VMEM)
HBM = pl.BlockSpec(memory_space=pltpu.HBM)
SMEM = pl.BlockSpec(memory_space=pltpu.SMEM)
PARAMS = pltpu.CompilerParams(vmem_limit_bytes=8 << 20)


def cost(flops):
    return pl.CostEstimate(flops=flops, bytes_accessed=0, transcendentals=0)


def at(start, size):
    return pl.ds(pl.multiple_of(start, size), size)


def local(densities, cluster_size, near_block, row_factor, column_factor):
    slots, loads = densities.shape
    groups = lax.axis_size("sub")
    regions = lax.axis_size("region")
    clusters = groups * regions
    rank = row_factor.shape[1] // clusters
    height = groups * rank
    width = (regions - 1) * rank
    bf16, f32 = jnp.bfloat16, jnp.float32
    hops = range(regions - 1, 0, -1)

    def ahead(sub, step):
        return lax.rem(sub + step, groups)

    def behind(sub, step):
        return lax.rem(sub + groups - step, groups)

    def across(region, hop):
        return lax.bitwise_xor(region, jnp.int32(hop))

    def gather(dens, col, *refs):
        outs, (dens_buf, col_buf, sems) = refs[: groups - 1], refs[groups - 1 :]
        sub = lax.axis_index("sub")
        region = lax.axis_index("region")
        first = pltpu.make_async_copy(dens, dens_buf, sems.at[0])
        copies = []
        for step in range(1, groups):
            goal = ahead(sub, step)
            copies.append(pltpu.make_async_copy(col.at[:, goal], col_buf.at[step - 1], sems.at[1]))
            copies[-1].start()
        first.start()
        first.wait()
        for out in outs:
            out[0:slots, :] = dens_buf[...]
        for copy in copies:
            copy.wait()
        for i, out in enumerate(outs):
            for hop in range(1, regions):
                low = slots + (hop - 1) * rank
                out[low : low + rank, :] = col_buf[i, across(region, hop)]

    parcels = pl.pallas_call(
        gather,
        out_shape=[jax.ShapeDtypeStruct((slots + width, loads), bf16)] * (groups - 1),
        in_specs=[HBM] * 2,
        out_specs=[VMEM] * (groups - 1),
        scratch_shapes=[
            pltpu.VMEM((slots, loads), bf16),
            pltpu.VMEM((groups - 1, regions, rank, slots), bf16),
            pltpu.SemaphoreType.DMA((2,)),
        ],
        compiler_params=PARAMS,
        name="gather",
    )(
        pltpu.with_memory_space_constraint(densities, pltpu.HBM),
        pltpu.with_memory_space_constraint(column_factor.reshape(regions, groups, rank, slots), pltpu.HBM),
    )

    held = []
    for step in range(1, groups):
        pairs = [(z, (z + step) % groups) for z in range(groups)]
        held.append(lax.ppermute(parcels[step - 1], "sub", pairs))

    def mask(size_ref, group_ref, own_ref):
        sub = lax.axis_index("sub")
        region = lax.axis_index("region")
        slot = lax.broadcasted_iota(jnp.int32, (slots, loads), 0)
        for g in range(groups):
            keep = slot < size_ref[region * groups + g]
            group_ref[g * slots : (g + 1) * slots, :] = jnp.where(keep, 1.0, 0.0).astype(bf16)
        own_ref[...] = jnp.where(slot < size_ref[region * groups + sub], 1.0, 0.0)

    group_mask, own_mask = pl.pallas_call(
        mask,
        out_shape=[
            jax.ShapeDtypeStruct((groups * slots, loads), bf16),
            jax.ShapeDtypeStruct((slots, loads), f32),
        ],
        in_specs=[SMEM],
        out_specs=[VMEM] * 2,
        compiler_params=PARAMS,
        cost_estimate=cost(1 << 20),
        name="mask",
    )(cluster_size)

    def weigh(step, mask_ref, parcel, outs):
        sub = lax.axis_index("sub")
        origin = behind(sub, step)
        rows = parcel[0:slots, :] * mask_ref[at(origin * slots, slots), :]
        part = jnp.dot(parcel[slots:, :], rows, preferred_element_type=f32).astype(bf16)
        for hop in range(1, regions):
            outs[hop - 1][at(origin * rank, rank), :] = part[(hop - 1) * rank : hop * rank, :]

    def regroup(mask_ref, dens_ref, col_ref, *refs):
        parcels, outs, own = refs[: groups - 2], refs[groups - 2 : -1], refs[-1]
        sub = lax.axis_index("sub")
        region = lax.axis_index("region")
        own[0:slots, :] = dens_ref[...]
        for hop in range(1, regions):
            low = slots + (hop - 1) * rank
            own[low : low + rank, :] = col_ref[across(region, hop), sub]
        for step, parcel in enumerate((own, *parcels)):
            weigh(step, mask_ref, parcel, outs)

    def complete(mask_ref, parcel, *refs):
        begun, outs = refs[: regions - 1], refs[regions - 1 :]
        for source, out in zip(begun, outs):
            out[...] = source[...]
        weigh(groups - 1, mask_ref, parcel, outs)

    letter_shapes = [jax.ShapeDtypeStruct((height, loads), bf16)] * (regions - 1)
    letters = pl.pallas_call(
        regroup,
        out_shape=letter_shapes,
        in_specs=[VMEM] * (groups + 1),
        out_specs=[VMEM] * (regions - 1),
        scratch_shapes=[pltpu.VMEM((slots + width, loads), bf16)],
        compiler_params=PARAMS,
        cost_estimate=cost(1 << 20),
        name="regroup",
    )(group_mask, densities, column_factor.reshape(regions, groups, rank, slots), *held[:-1])
    letters = pl.pallas_call(
        complete,
        out_shape=letter_shapes,
        in_specs=[VMEM] * (regions + 1),
        out_specs=[VMEM] * (regions - 1),
        compiler_params=PARAMS,
        cost_estimate=cost(1 << 20),
        name="complete",
    )(group_mask, held[-1], *letters)

    received = {}
    for hop in hops:
        pairs = [(r, r ^ hop) for r in range(regions)]
        received[hop] = lax.ppermute(letters[hop - 1], "region", pairs)

    late = min(2, regions - 1)
    early = [hop for hop in range(1, regions) if hop != late]

    def far_part(factor_ref, letter, hop):
        start = across(lax.axis_index("region"), hop) * height
        return jnp.dot(factor_ref[:, at(start, height)], letter[...], preferred_element_type=f32)

    def near(block_ref, mask_ref, *refs):
        parcels, out, stack = refs[:groups], refs[groups], refs[groups + 1]
        sub = lax.axis_index("sub")
        for step in range(groups):
            here = at(behind(sub, step) * slots, slots)
            stack[here, :] = parcels[step][0:slots, :] * mask_ref[here, :]
        out[...] = jnp.dot(block_ref[...], stack[...], preferred_element_type=f32)

    near_sum = pl.pallas_call(
        near,
        out_shape=jax.ShapeDtypeStruct((slots, loads), f32),
        in_specs=[VMEM] * (groups + 2),
        out_specs=VMEM,
        scratch_shapes=[pltpu.VMEM((groups * slots, loads), bf16)],
        compiler_params=PARAMS,
        cost_estimate=cost(1 << 24),
        name="near",
    )(near_block, group_mask, densities, *held)

    def gain(near_ref, factor_ref, *refs):
        total = near_ref[...]
        for hop, letter in zip(early, refs):
            total += far_part(factor_ref, letter, hop)
        refs[-1][...] = total

    partial = pl.pallas_call(
        gain,
        out_shape=jax.ShapeDtypeStruct((slots, loads), f32),
        in_specs=[VMEM] * (len(early) + 2),
        out_specs=VMEM,
        compiler_params=PARAMS,
        cost_estimate=cost(1 << 24),
        name="gain",
    )(near_sum, row_factor, *(received[hop] for hop in early))

    def finish(mask_ref, partial_ref, factor_ref, letter, out):
        total = partial_ref[...] + far_part(factor_ref, letter, late)
        out[...] = jnp.where(mask_ref[...] > 0.0, total, 0.0)

    return pl.pallas_call(
        finish,
        out_shape=jax.ShapeDtypeStruct((slots, loads), f32),
        in_specs=[VMEM] * 4,
        out_specs=VMEM,
        compiler_params=PARAMS,
        cost_estimate=cost(1 << 24),
        name="finish",
    )(own_mask, partial, row_factor, received[late])


def solution(mesh):
    spec = P(("sample", "region", "sub"), None)
    return jax.shard_map(
        local,
        mesh=mesh,
        in_specs=(spec, P("sample"), spec, spec, P(None, ("sample", "region", "sub"))),
        out_specs=spec,
        check_vma=False,
    )
```
